32 devices in a mesh: ep: 8 (over z, x), tp: 4 (over y, core).
Axes of the slice: x: 2, y: 2, z: 4, core: 2. Of those that a mesh axis runs over, the one named last changes fastest.
Arguments:
- hidden_in: bfloat16 [1024, 2048], P('ep', 'tp'), may hold values from -6 to 6
- norm_gain: float32 [2048], replicated, may hold values from 0.5 to 1.5
- router_weight: bfloat16 [2048, 8], replicated, may hold values from -4.861359 to 4.861359
- shared_gate_up: bfloat16 [2048, 2, 1408], P(None, None, 'tp'), may hold values from -0.125 to 0.125
- shared_down: bfloat16 [1408, 2048], P('tp'), may hold values from -0.15625 to 0.15625
- slot_gate_up: bfloat16 [32, 2048, 2, 704], P(('ep', 'tp')), as said below
- slot_down: bfloat16 [32, 704, 2048], P(('ep', 'tp')), as said below
- slot_expert: int32 [32], replicated, may hold values from 0 to 7, as said below
- slot_choice: int32 [1024, 6], P('ep'), may hold values from 0 to 31, all different within a row; in each aligned block of 32 rows (0 to 31, 32 to 63, ...) at most 12 rows name the same one
- live_count: int32 [8], P('ep'), may hold values from 64 to 128, as said below
Outputs:
- mixed_out: bfloat16 [1024, 2048], P('ep', 'tp')
The draws below stay inside these ranges and needn't reach their ends.
Inputs may be any that keep to these rules, and one draw needn't show every extreme that they name: `slot_expert`: each expert is held by 1 or 7 slots; exactly 4 experts by the larger number. `slot_gate_up`: entry s holds the weights of expert slot_expert[s]; slots of one expert hold equal weights. `slot_down`: entry s holds the weights of expert slot_expert[s]; slots of one expert hold equal weights. `slot_choice`: a row names 6 different slots; in each aligned block of 32 rows no slot is named more than 12 times. `live_count`: the live rows of an index of ep are its first ones; some index of ep has all 128 rows live.
All inputs are finite; a program needn't handle non-finite values.
Results may differ from the reference program's by a relative error of at most 0.0058.
Values may be sent and summed in bfloat16 or wider, within the bound.
A program may use at most 64 MiB of HBM per device.

```python
import math
import jax
import jax.numpy as jnp
import numpy as np
from jax import lax

D = 2048
EXP_FF = 704
SHARED_FF = 1408
TOP = 6
TOK_DEV = 128
EXPERTS = 8
SLOTS = 32
CAP = 12
TOKENS = 1024
N_EP = 8
N_TP = 4


def placement_table(key):
    copies = 2 * (SLOTS // EXPERTS) - 1
    shuffled = jax.random.permutation(jax.random.fold_in(key, 11), EXPERTS).astype(jnp.int32)
    hot_half = shuffled[:EXPERTS // 2]
    listed = jnp.concatenate([jnp.tile(hot_half, copies), shuffled[EXPERTS // 2:]])
    mixing = jax.random.permutation(jax.random.fold_in(key, 12), SLOTS)
    return listed[mixing].astype(jnp.int32)


def expert_block(weight_key, expert, shape, fan_in):
    sub_key = jax.random.fold_in(weight_key, expert)
    values = jax.random.normal(sub_key, shape, jnp.float32)
    return (values * fan_in ** (-0.5)).astype(jnp.bfloat16)


def draw_slot_expert(key, part):
    return placement_table(key)


def draw_slot_gate_up(key, part):
    slot_table = placement_table(key)
    weight_key = jax.random.fold_in(key, 21)
    return lax.map(lambda expert: expert_block(weight_key, expert, (D, 2, EXP_FF), D), slot_table)


def draw_slot_down(key, part):
    slot_table = placement_table(key)
    weight_key = jax.random.fold_in(key, 22)
    return lax.map(lambda expert: expert_block(weight_key, expert, (EXP_FF, D), EXP_FF), slot_table)


def draw_router_weight(key, part):
    base = jax.random.normal(jax.random.fold_in(key, 31), (D, EXPERTS), jnp.float32)
    column_scale = jnp.exp(jax.random.uniform(jax.random.fold_in(key, 34), (EXPERTS,), jnp.float32, -1.2, 0.0))
    matrix = base * column_scale
    return (matrix * D ** (-0.5)).astype(jnp.bfloat16)


def draw_live_count(key, part):
    counts = jax.random.randint(jax.random.fold_in(key, 41), (N_EP,), TOK_DEV // 2, TOK_DEV + 1)
    fullest = jax.random.randint(jax.random.fold_in(key, 42), (), 0, N_EP)
    return jnp.where(jnp.arange(N_EP) == fullest, TOK_DEV, counts).astype(jnp.int32)


def levels(key, shape, cuts, smallest, top_value):
    loudness = 1.0
    for dim, blocks in cuts:
        draws = jax.random.uniform(jax.random.fold_in(jax.random.fold_in(key, 6), dim), (blocks,), jnp.float32, smallest / len(cuts), top_value / len(cuts))
        loudness = loudness * jnp.repeat(jnp.exp(draws), shape[dim] // blocks).reshape((-1,) + (1,) * (len(shape) - 1 - dim))
    return loudness


def assign_block(key, own, number, rows, amount, top, most, slope):
    ranking = jax.random.permutation(key, amount)
    crowded, usual = shares(amount, rows * top, most, slope, True), shares(amount, rows * top, most, slope, False)
    places = jnp.arange(amount)

    def named(tallies, offset_by):
        used = int((tallies > 0).sum())
        fixed = max(1, used // 4)
        passed = fixed + (places - fixed + offset_by * (used - fixed)) % max(1, amount - fixed)
        return jnp.zeros((amount,), jnp.int32).at[ranking[jnp.where(places < fixed, places, passed)]].set(jnp.asarray(tallies, jnp.int32))

    tallies = jnp.where(number % 4 == 0, named(crowded, number // 4), named(usual, number - number // 4 - 1))
    mixed = jax.random.permutation(jax.random.fold_in(own, 3), amount)
    source_of, receiver = mixed[0:amount // 2 * 2:2], mixed[1:amount // 2 * 2:2]
    margin = jnp.minimum(tallies[source_of] - 1, most - tallies[receiver]) // 2
    margin = jnp.where((source_of == ranking[0]) | (receiver == ranking[0]) | (tallies[receiver] == 0), 0, jnp.maximum(margin, 0))
    passed = jax.random.randint(jax.random.fold_in(own, 4), (amount // 2,), 0, 1 << 20) % (margin + 1)
    tallies = tallies.at[source_of].add(-passed).at[receiver].add(passed)
    items = jnp.searchsorted(jnp.cumsum(tallies), jnp.arange(rows * top), side="right").astype(jnp.int32)
    grid = items.reshape(top, rows).T
    grid = grid[jax.random.permutation(jax.random.fold_in(own, 1), rows)]
    offset_by = jax.random.randint(jax.random.fold_in(own, 2), (rows, 1), 0, top)
    return jnp.take_along_axis(grid, (jnp.arange(top)[None, :] + offset_by) % top, axis=1)


def shares(number_of, total, reach, slope, full):
    portions = [(1 << 20) // math.isqrt(rank ** slope) + 1 for rank in range(1, number_of + 1)]
    largest = reach if full else min(reach, max(-(-total // number_of), total * portions[0] // sum(portions)))
    least = 1 if total - largest >= number_of - 1 else 0
    given, surplus = [largest] + [least] * (number_of - 1), total - largest - least * (number_of - 1)
    while surplus > 0:
        free = [i for i in range(1, number_of) if given[i] < largest] or [i for i in range(1, number_of) if given[i] < reach]
        whole, remaining = sum([portions[i] for i in free]), surplus
        for i in free:
            more = min(reach - given[i], max(1, remaining * portions[i] // whole), surplus)
            given[i] = given[i] + more
            surplus = surplus - more
    return np.array(given)


def noise(stream_key, extent, deviation, bound, split=(), held_as=jnp.bfloat16):
    drawn = deviation * jax.random.normal(stream_key, extent, jnp.float32)
    if split:
        drawn = drawn * levels(stream_key, extent, split, -0.22, 0.18)
    return jnp.clip(drawn, -bound, bound).astype(held_as)


def setup_inputs(seed: int = 0) -> dict:
    streams_of = jax.random.split(jax.random.key(seed), 11)
    hidden_in = noise(streams_of[0], (TOKENS, D), 1.0, 6.0, ((0, 8), (1, 4)))
    norm_gain = jnp.clip(1.0 + 0.1 * jax.random.normal(streams_of[1], (D,), jnp.float32), 0.5, 1.5)
    router_weight = draw_router_weight(jax.random.fold_in(streams_of[10], 71), 0)
    shared_gate_up = noise(streams_of[3], (D, 2, SHARED_FF), D ** -0.5, 0.125, ((2, 4),))
    shared_down = noise(streams_of[4], (SHARED_FF, D), SHARED_FF ** -0.5, 0.15625, ((0, 4),))
    slot_gate_up = draw_slot_gate_up(jax.random.fold_in(streams_of[10], 71), 0)
    slot_down = draw_slot_down(jax.random.fold_in(streams_of[10], 71), 0)
    slot_expert = draw_slot_expert(jax.random.fold_in(streams_of[10], 71), 0)
    slot_choice_keys = jax.random.split(jax.random.fold_in(streams_of[8], 1), TOKENS // (TOK_DEV // N_TP))
    slot_choice_turns = jax.random.permutation(jax.random.fold_in(streams_of[8], 3), TOKENS // (TOK_DEV // N_TP))
    slot_choice = jax.vmap(lambda own, number: assign_block(jax.random.fold_in(streams_of[8], 2), own, number, TOK_DEV // N_TP, SLOTS, TOP, CAP, 2))(slot_choice_keys, slot_choice_turns).reshape((TOKENS, TOP))
    live_count = draw_live_count(jax.random.fold_in(streams_of[10], 71), 0)
    return dict(hidden_in=hidden_in, norm_gain=norm_gain, router_weight=router_weight, shared_gate_up=shared_gate_up, shared_down=shared_down, slot_gate_up=slot_gate_up, slot_down=slot_down, slot_expert=slot_expert, slot_choice=slot_choice, live_count=live_count)


def reference(hidden_in, norm_gain, router_weight, shared_gate_up, shared_down, slot_gate_up, slot_down, slot_expert, slot_choice, live_count):
    wide_rows = hidden_in.astype(jnp.float32)
    norm_scale = lax.rsqrt(lax.optimization_barrier(jnp.mean(wide_rows * wide_rows, axis=1, keepdims=True)) + 1e-06)
    normed = (wide_rows * norm_scale * norm_gain).astype(jnp.bfloat16)
    logits = jnp.dot(normed, router_weight, preferred_element_type=jnp.float32)
    expert_ids = slot_expert[slot_choice].astype(jnp.int32)
    picked = jnp.take_along_axis(logits, expert_ids, axis=1)
    gate_values = jax.nn.softmax(picked, axis=1).astype(jnp.bfloat16)
    shared_proj = jnp.einsum('td,dgf->tgf', normed.astype(jnp.float32), shared_gate_up.astype(jnp.float32))
    shared_hidden = (jax.nn.silu(shared_proj[:, 0]) * shared_proj[:, 1]).astype(jnp.bfloat16)
    shared_out = jnp.dot(shared_hidden.astype(jnp.float32), shared_down.astype(jnp.float32), preferred_element_type=jnp.float32)
    depth = TOKENS // (TOK_DEV // N_TP) * CAP
    flat_slots = slot_choice.reshape(-1).astype(jnp.int32)
    ordering = jnp.argsort(flat_slots, stable=True).astype(jnp.int32)
    sorted_slots = flat_slots[ordering]
    slot_range = jnp.arange(SLOTS, dtype=jnp.int32)
    firsts = jnp.searchsorted(sorted_slots, slot_range, side='left').astype(jnp.int32)
    lasts = jnp.searchsorted(sorted_slots, slot_range, side='right').astype(jnp.int32)
    padded_order = jnp.concatenate([ordering, jnp.zeros((depth,), jnp.int32)])
    flat_gates = gate_values.reshape(-1).astype(jnp.float32)

    def visit_slot(routed_sum, slot_index):
        pick_ids = lax.dynamic_slice_in_dim(padded_order, firsts[slot_index], depth)
        in_range = jnp.arange(depth, dtype=jnp.int32) < lasts[slot_index] - firsts[slot_index]
        token_ids = (pick_ids // TOP).astype(jnp.int32)
        inputs = normed[token_ids].astype(jnp.float32)
        gate_up = jnp.einsum('rd,dgf->rgf', inputs, slot_gate_up[slot_index].astype(jnp.float32))
        activated = (jax.nn.silu(gate_up[:, 0]) * gate_up[:, 1]).astype(jnp.bfloat16)
        result = jnp.dot(activated.astype(jnp.float32), slot_down[slot_index].astype(jnp.float32), preferred_element_type=jnp.float32).astype(jnp.bfloat16)
        weight = jnp.where(in_range, flat_gates[pick_ids], jnp.zeros_like(flat_gates[pick_ids]))
        routed_sum = routed_sum.at[token_ids].add(weight[:, None] * result.astype(jnp.float32))
        return (routed_sum, None)
    routed_pair = lax.scan(visit_slot, jnp.zeros((TOKENS, D), jnp.float32), slot_range)
    routed = routed_pair[0]
    positions = jnp.arange(TOKENS, dtype=jnp.int32)
    live_rows = positions % TOK_DEV < live_count[positions // TOK_DEV]
    mixed_out = jnp.where(live_rows[:, None], wide_rows + shared_out + routed, jnp.zeros_like(routed))
    return mixed_out.astype(jnp.bfloat16)
```

```python
import functools
import jax
import jax.numpy as jnp
from jax import lax
from jax.experimental import pallas as pl
from jax.experimental.pallas import tpu as pltpu
from jax.sharding import PartitionSpec as P


def gate_weights(normed_rows, choices, router_weight, slot_expert):
    logits = jnp.dot(normed_rows, router_weight, preferred_element_type=jnp.float32)
    slot_total = slot_expert.shape[0]
    expert_total = router_weight.shape[1]
    slot_hit = choices[:, :, None] == jnp.arange(slot_total, dtype=jnp.int32)
    expert_ids = jnp.sum(jnp.where(slot_hit, slot_expert, 0), axis=2)
    expert_hit = expert_ids[:, :, None] == jnp.arange(expert_total, dtype=jnp.int32)
    picked = jnp.sum(jnp.where(expert_hit, logits[:, None, :], 0.0), axis=2)
    highest = jnp.max(picked, axis=1, keepdims=True)
    weights = jnp.exp(picked - highest)
    return (weights / jnp.sum(weights, axis=1, keepdims=True)).astype(jnp.bfloat16)


def slot_positions(targets):
    length = targets.shape[0]
    same_slot = targets[:, None] == targets[None, :]
    earlier = jnp.arange(length)[None, :] < jnp.arange(length)[:, None]
    return jnp.sum(same_slot & earlier, axis=1)


def expert_apply(received, slot_gate_up, slot_down):
    shape_in = received.shape
    flat_rows = received.reshape(-1, shape_in[-1])
    gate_up = jnp.einsum(
        "rd,dgf->rgf", flat_rows, slot_gate_up[0], preferred_element_type=jnp.float32
    )
    activated = (jax.nn.silu(gate_up[:, 0]) * gate_up[:, 1]).astype(jnp.bfloat16)
    result = jnp.dot(activated, slot_down[0], preferred_element_type=jnp.float32).astype(
        jnp.bfloat16
    )
    return result.reshape(shape_in)


def local_exchange(
    hidden_in,
    norm_gain,
    router_weight,
    shared_gate_up,
    shared_down,
    slot_gate_up,
    slot_down,
    slot_expert,
    slot_choice,
    live_count,
):
    tp_count = lax.axis_size("tp")
    ep_count = lax.axis_size("ep")
    tp_index = lax.axis_index("tp")
    tok_count = hidden_in.shape[0]
    feature_width = hidden_in.shape[1] * tp_count
    top_count = slot_choice.shape[1]
    slot_count = slot_expert.shape[0]
    quarter = tok_count // tp_count
    capacity = max(2, 2 * quarter * top_count // slot_count)
    full_rows = lax.all_gather(hidden_in, "tp", axis=1, tiled=True)
    wide_rows = full_rows.astype(jnp.float32)
    norm_scale = lax.rsqrt(jnp.mean(wide_rows * wide_rows, axis=1, keepdims=True) + 1e-06)
    normed = (wide_rows * norm_scale * norm_gain).astype(jnp.bfloat16)
    shared_proj = jnp.einsum(
        "td,dgf->tgf", normed, shared_gate_up, preferred_element_type=jnp.float32
    )
    shared_hidden = (jax.nn.silu(shared_proj[:, 0]) * shared_proj[:, 1]).astype(jnp.bfloat16)
    partial_value = jnp.dot(shared_hidden, shared_down, preferred_element_type=jnp.float32)
    row_start = tp_index * quarter
    own_rows = lax.dynamic_slice_in_dim(normed, row_start, quarter, 0)
    own_choice = lax.dynamic_slice_in_dim(slot_choice, row_start, quarter, 0)
    gate_values = gate_weights(own_rows, own_choice, router_weight, slot_expert)
    targets = own_choice.reshape(-1)
    placed = targets * capacity + slot_positions(targets)
    outgoing = jnp.zeros((slot_count * capacity, feature_width), jnp.bfloat16)
    outgoing = outgoing.at[placed].set(jnp.repeat(own_rows, top_count, axis=0))
    outgoing = outgoing.reshape(ep_count, tp_count, capacity, feature_width)
    arrived = lax.all_to_all(
        lax.all_to_all(outgoing, "ep", split_axis=0, concat_axis=0, tiled=True),
        "tp",
        split_axis=1,
        concat_axis=1,
        tiled=True,
    )
    computed = expert_apply(arrived, slot_gate_up, slot_down)
    returned = lax.all_to_all(
        lax.all_to_all(computed, "ep", split_axis=0, concat_axis=0, tiled=True),
        "tp",
        split_axis=1,
        concat_axis=1,
        tiled=True,
    )
    fetched = returned.reshape(-1, feature_width)[placed].reshape(quarter, top_count, feature_width)
    routed = jnp.einsum("qk,qkd->qd", gate_values, fetched, preferred_element_type=jnp.float32)
    own_partial = lax.dynamic_slice_in_dim(partial_value, row_start, quarter, 0) + routed
    partial_value = lax.dynamic_update_slice_in_dim(partial_value, own_partial, row_start, 0)
    summed = lax.psum_scatter(partial_value, "tp", scatter_dimension=1, tiled=True)
    live_rows = jnp.arange(tok_count, dtype=jnp.int32) < live_count[0]
    mixed_out = jnp.where(live_rows[:, None], hidden_in.astype(jnp.float32) + summed, 0.0)
    return mixed_out.astype(jnp.bfloat16)


def dot_nt(a, b):
    return lax.dot_general(a, b, (((1,), (1,)), ((), ())), preferred_element_type=jnp.float32)


def dot_nn(a, b):
    return jnp.dot(a, b, preferred_element_type=jnp.float32)


def silu_mul(g, u):
    return (g / (1.0 + jnp.exp(-g)) * u).astype(jnp.bfloat16)


def chunks(total, step):
    return [(at, min(step, total - at)) for at in range(0, total, step)]


def plane_kernel(
    rows_max,
    slot_cap,
    top,
    hid,
    ch_own,
    slot_row,
    gain,
    router_t,
    w_gu,
    w_d,
    w_sgu,
    w_sd,
    out,
    zbuf,
    cz,
    gz,
    mz,
    shx,
    held,
    place,
    psel,
    sbuf,
    rbuf,
    gu,
    dn,
    sgu,
    sdn,
    own,
    hsh,
    shp,
    ssnd,
    srecv,
    sysnd,
    sy,
    sel,
    hmid,
    eo,
    ec,
    ro,
    ret,
    osum,
    rz,
    own_sum,
    wsem,
    ssem,
    rsem,
):
    bf16, f32 = jnp.bfloat16, jnp.float32
    ep, tp = lax.axis_index("ep"), lax.axis_index("tp")
    z, x, y, c = ep // 2, ep % 2, tp // 2, tp % 2
    tok, width = hid.shape
    feat = gain.shape[1]
    slots = slot_row.shape[1]
    experts_total = router_t.shape[0]
    reach = rows_max
    planes = (z, z + 1 - 2 * (z % 2), (z + 2) % 4, 3 - z)

    def at_ep(m, i):
        return planes[m] * 2 + (1 - x if i else x)

    def at_tp(k, l):
        return (1 - y if k else y) * 2 + (1 - c if l else c)

    def cols(k, l):
        return pl.ds(pl.multiple_of(at_tp(k, l) * width, width), width)

    chips = [(0, 0), (0, 1), (1, 0), (1, 1)]
    c_dev = (ep, at_tp(0, 1))
    chip_dev = {(i, k): (at_ep(0, i), at_tp(k, 0)) for i, k in chips}
    z_dev = [(at_ep(m, 0), tp) for m in range(4)]

    loads = [
        pltpu.make_async_copy(src, dst, wsem.at[n])
        for n, (src, dst) in enumerate(((w_sgu, sgu), (w_sd, sdn), (w_gu, gu), (w_d, dn)))
    ]
    barrier = pltpu.get_barrier_semaphore()
    greeted = [c_dev] + [chip_dev[q] for q in chips[1:]] + z_dev[1:]
    for dev in greeted:
        pl.semaphore_signal(barrier, inc=1, device_id=dev, device_id_type=pl.DeviceIdType.MESH)

    z_order = (1, 2, 3)
    copies = {}

    def send(name, src, dst, dev):
        n = len(copies)
        copy = pltpu.make_async_remote_copy(
            src_ref=src,
            dst_ref=dst,
            send_sem=ssem.at[n],
            recv_sem=rsem.at[n],
            device_id=dev,
            device_id_type=pl.DeviceIdType.MESH,
        )
        copy.start()
        copies[name] = copy

    def got(*name):
        copies[name].wait_recv()

    def one_hot(test):
        return jnp.where(test, 1.0, 0.0).astype(bf16)

    def tables():
        kind = lax.broadcasted_iota(jnp.int32, (experts_total, slots), 0)
        table = jnp.where(slot_row[...] == kind, 1.0, 0.0)
        copies_of = jnp.sum(table, axis=1, keepdims=True)
        single = jnp.sum(jnp.where(copies_of < 1.5, table, 0.0), axis=0, keepdims=True)
        a = lax.broadcasted_iota(jnp.int32, (slots, slots), 0)
        b = lax.broadcasted_iota(jnp.int32, (slots, slots), 1)
        single8 = jnp.broadcast_to(single, (8, slots))
        beside = dot_nn(single8.astype(bf16), one_hot(a == b + 1 - 2 * (b & 1)))
        share = jnp.where(
            single8 > 0.5,
            float(slot_cap),
            jnp.where(beside > 0.5, float(reach - slot_cap), float(reach // 2)),
        )
        table = table.astype(bf16)
        same = lax.dot_general(
            table, table, (((0,), (0,)), ((), ())), preferred_element_type=f32
        )
        first = dot_nn(share.astype(bf16), jnp.where(a < b, same, 0.0).astype(bf16))[0:1, :]
        share = share[0:1, :]
        slot = lax.broadcasted_iota(jnp.int32, (reach, slots), 1)
        start = jnp.where((slot & 1) == 1, float(reach) - share, 0.0)
        row = lax.broadcasted_iota(jnp.int32, (reach, slots), 0).astype(f32)
        inside = (row >= start) & (row < start + share)
        mine = None
        for n, (i, k) in enumerate(chips):
            even = at_ep(0, i) * 4 + (1 - y if k else y) * 2
            named = inside & ((slot == even) | (slot == even + 1))
            held[n * reach : (n + 1) * reach, :] = dot_nt(one_hot(named), table).astype(bf16)
            place[n * reach : (n + 1) * reach, :] = jnp.sum(
                jnp.where(named, first + row - start, 0.0), axis=1, keepdims=True
            )
            if n == 0:
                mine = jnp.sum(
                    jnp.where(named & (slot == even + c), 1.0, 0.0), axis=1, keepdims=True
                )
        return table, mine

    def choose(m, table):
        picks = ch_own[...] if m == 0 else cz[m]
        slot_ids = lax.broadcasted_iota(jnp.int32, (slots, tok), 0)
        named = jnp.zeros((slots, tok), f32)
        for k in range(top):
            named = jnp.where(picks[k : k + 1, :] == slot_ids, 1.0, named)
        times = dot_nn(table, named.astype(bf16))
        earlier = one_hot(
            lax.broadcasted_iota(jnp.int32, (tok, tok), 0)
            < lax.broadcasted_iota(jnp.int32, (tok, tok), 1)
        )
        rank = dot_nn(one_hot(times > 0.5), earlier)
        rank = jnp.where(times > 0.5, rank, -1.0).astype(bf16)
        mz[m] = times
        psel[m] = one_hot(dot_nn(held[...], rank) == place[...])

    def pick(m):
        src = hid if m == 0 else zbuf.at[m]
        for n in (1, 2, 3, 0):
            if m == 0 and n < 2:
                continue
            sbuf[m, n] = dot_nn(psel[m, n * reach : (n + 1) * reach, :], src[...]).astype(bf16)
            if m:
                ship(m, n)

    def ship(m, n):
        i, k = chips[n]
        if n:
            send(("g", m, n), sbuf.at[m, n], rbuf.at[m, n, 0], chip_dev[i, k])
        else:
            send(("gc", m, n), sbuf.at[m, 0], rbuf.at[m, 0, 1], c_dev)

    def norm_scale(*parts):
        squares = sum(jnp.sum(v * v, axis=1, keepdims=True) for v in parts)
        return lax.rsqrt(squares * (1.0 / feat) + 1e-06)

    def normed(refs, keep=None):
        parts = {kl: ref[...].astype(f32) for kl, ref in refs.items()}
        scale = norm_scale(*parts.values())
        if keep is not None:
            scale = scale * keep
        for (k, l), v in parts.items():
            yield k, l, (v * scale * gain[:, cols(k, l)]).astype(bf16)

    def own_rows():
        got("sc")
        got("sy")
        send(("syc",), shx.at[1], shx.at[2], c_dev)

    def own_norm():
        got("syc")
        for k, l, v in normed({(0, 0): hid, (0, 1): shx.at[0], (1, 0): shx.at[1], (1, 1): shx.at[2]}):
            own[:, cols(k, l)] = v

    def gates():
        logits = dot_nt(router_t[...], own[...])
        times = mz[0]
        there = times > 0.5
        top_logit = jnp.max(jnp.where(there, logits, -1e30), axis=0, keepdims=True)
        weights = jnp.where(there, jnp.exp(jnp.where(there, logits - top_logit, 0.0)), 0.0)
        total = jnp.sum(weights * times, axis=0, keepdims=True)
        gz[0] = (weights / total).astype(bf16).astype(f32)
        for m in (1, 2, 3):
            send(("gate", m), gz.at[0], gz.at[m], z_dev[m])

    def shared():
        loads[0].wait()
        ff = hsh.shape[1]
        hsh[...] = silu_mul(dot_nt(own[...], sgu[0:ff, :]), dot_nt(own[...], sgu[ff : 2 * ff, :]))
        loads[1].wait()
        for k in (0, 1):
            ssnd[k] = dot_nn(hsh[...], sdn[:, cols(k, 1)]).astype(bf16)
        send(("shc",), ssnd, srecv, c_dev)
        for k in (0, 1):
            shp[k] = dot_nn(hsh[...], sdn[:, cols(k, 0)])

    def shared_pass():
        got("shc")
        sysnd[...] = (shp[1] + srecv[1].astype(f32)).astype(bf16)
        send(("shy",), sysnd, sy, chip_dev[0, 1])
        own_sum[...] = hid[...].astype(f32) + shp[0] + srecv[0].astype(f32)

    def forward(m):
        for n in (1, 2, 3):
            if m == 0 and n == 1:
                continue
            got("g", m, n)
            send(("gc", m, n), rbuf.at[m, n, 0], rbuf.at[m, n, 1], c_dev)

    pos = {m: n for n, m in enumerate((0,) + z_order)}
    span = 2 * reach

    def prepare(m, mine):
        for i in (0, 1):
            at = slice(pos[m] * span + i * reach, pos[m] * span + (i + 1) * reach)
            if m == 0 and i == 0:
                chosen = (psel[m, 0:reach, :].astype(f32) * mine).astype(bf16)
                for lo, size in chunks(feat, 512):
                    sel[at, lo : lo + size] = dot_nn(chosen, own[:, lo : lo + size]).astype(bf16)
                continue
            refs = {}
            for k in (0, 1):
                n = 2 * i + k
                refs[k, 0] = rbuf.at[m, n, 0] if n else sbuf.at[m, 0]
                got("gc", m, n)
                refs[k, 1] = rbuf.at[m, n, 1]
            for k, l, v in normed(refs, mine):
                sel[at, cols(k, l)] = v

    def experts(ms):
        part = slice(pos[ms[0]] * span, (pos[ms[-1]] + 1) * span)
        if ms[0] == 0:
            loads[2].wait()
        ff = hmid.shape[1]
        for at, size in chunks(ff, 256):
            hmid[part, at : at + size] = silu_mul(
                dot_nt(sel[part, :], gu[at : at + size, :]),
                dot_nt(sel[part, :], gu[ff + at : ff + at + size, :]),
            )
        if ms[0] == 0:
            loads[3].wait()
        for l in (1, 0):
            for k in (0, 1):
                value = dot_nn(hmid[part, :], dn[:, cols(k, l)]).astype(bf16)
                for n, m in enumerate(ms):
                    eo[m, l, k] = value[n * span : (n + 1) * span, :]
            if l:
                for m in ms:
                    send(("ec", m), eo.at[m, 1], ec.at[m], c_dev)

    def give_back(m):
        got("ec", m)
        for n in (3, 2, 1, 0):
            i, k = chips[n]
            at = slice(i * reach, (i + 1) * reach)
            value = eo[m, 0, k, at, :] + ec[m, k, at, :]
            if n:
                ro[m, n] = value
                send(("r", m, n), ro.at[m, n], ret.at[m, n], chip_dev[i, k])
            else:
                ret[m, 0] = value

    def collect(m):
        if m:
            got("gate", m)
        weight = dot_nn(held[...], gz[m].astype(bf16)) * dot_nn(held[...], mz[m].astype(bf16))
        weight = (weight * psel[m].astype(f32)).astype(bf16)
        for n in (1, 2, 3):
            got("r", m, n)
        part = lax.dot_general(
            weight,
            ret[m].reshape(4 * reach, width),
            (((0,), (0,)), ((), ())),
            preferred_element_type=f32,
        )
        if m:
            osum[m] = part.astype(bf16)
            send(("rz", m), osum.at[m], rz.at[m], z_dev[m])
        else:
            own_sum[...] += part

    for load in loads:
        load.start()
    table, mine = tables()
    choose(0, table)
    pick(0)
    pl.semaphore_wait(barrier, len(greeted))
    for m in z_order:
        send(("ch", m), ch_own, cz.at[m], z_dev[m])
    for m in z_order:
        send(("z", m), hid, zbuf.at[m], z_dev[m])
    send(("sy",), hid, shx.at[1], chip_dev[0, 1])
    send(("sc",), hid, shx.at[0], c_dev)
    ship(0, 3)
    ship(0, 2)
    for m in z_order:
        got("ch", m)
        choose(m, table)
    own_rows()
    a, b, d = z_order
    got("z", a)
    pick(a)
    own_norm()
    gates()
    shared()
    got("z", b)
    pick(b)
    forward(0)
    shared_pass()
    prepare(0, mine)
    forward(a)
    prepare(a, mine)
    got("z", d)
    pick(d)
    forward(b)
    prepare(b, mine)
    experts((0, a, b))
    give_back(a)
    give_back(b)
    forward(d)
    prepare(d, mine)
    experts((d,))
    give_back(d)
    give_back(0)
    collect(a)
    collect(b)
    collect(d)
    collect(0)
    got("shy")
    for m in z_order:
        got("rz", m)
    total = own_sum[...] + sy[...].astype(f32)
    for m in z_order:
        total = total + rz[m].astype(f32)
    out[...] = total.astype(bf16)
    for copy in copies.values():
        copy.wait_send()


def local_plane(
    rows_max,
    number,
    hidden_in,
    norm_gain,
    router_weight,
    shared_gate_up,
    shared_down,
    slot_gate_up,
    slot_down,
    slot_expert,
    slot_choice,
):
    tok_count, width = hidden_in.shape
    feat = 4 * width
    top_count = slot_choice.shape[1]
    slot_count = slot_expert.shape[0]
    expert_count = router_weight.shape[1]
    cap = 4 * max(2, 2 * (tok_count // 4) * top_count // slot_count)
    sff, eff = shared_down.shape[0], slot_down.shape[1]
    bf16, f32 = jnp.bfloat16, jnp.float32
    block = (tok_count, width)
    piece = (rows_max, width)
    vmem = pl.BlockSpec(memory_space=pltpu.VMEM)
    hbm = pl.BlockSpec(memory_space=pl.ANY)
    copy_count = 61
    return pl.pallas_call(
        functools.partial(plane_kernel, rows_max, cap, top_count),
        out_shape=jax.ShapeDtypeStruct(block, bf16),
        in_specs=[vmem] * 5 + [hbm] * 4,
        out_specs=vmem,
        scratch_shapes=[
            pltpu.VMEM((4,) + block, bf16),
            pltpu.VMEM((4, top_count, tok_count), jnp.int32),
            pltpu.VMEM((4, expert_count, tok_count), f32),
            pltpu.VMEM((4, expert_count, tok_count), f32),
            pltpu.VMEM((3,) + block, bf16),
            pltpu.VMEM((4 * rows_max, expert_count), bf16),
            pltpu.VMEM((4 * rows_max, 1), f32),
            pltpu.VMEM((4, 4 * rows_max, tok_count), bf16),
            pltpu.VMEM((4, 4) + piece, bf16),
            pltpu.VMEM((4, 4, 2) + piece, bf16),
            pltpu.VMEM((2 * eff, feat), bf16),
            pltpu.VMEM((eff, feat), bf16),
            pltpu.VMEM((2 * sff, feat), bf16),
            pltpu.VMEM((sff, feat), bf16),
            pltpu.VMEM((tok_count, feat), bf16),
            pltpu.VMEM((tok_count, sff), bf16),
            pltpu.VMEM((2,) + block, f32),
            pltpu.VMEM((2,) + block, bf16),
            pltpu.VMEM((2,) + block, bf16),
            pltpu.VMEM(block, bf16),
            pltpu.VMEM(block, bf16),
            pltpu.VMEM((8 * rows_max, feat), bf16),
            pltpu.VMEM((8 * rows_max, eff), bf16),
            pltpu.VMEM((4, 2, 2, 2 * rows_max, width), bf16),
            pltpu.VMEM((4, 2, 2 * rows_max, width), bf16),
            pltpu.VMEM((4, 4) + piece, bf16),
            pltpu.VMEM((4, 4) + piece, bf16),
            pltpu.VMEM((4,) + block, bf16),
            pltpu.VMEM((4,) + block, bf16),
            pltpu.VMEM(block, f32),
            pltpu.SemaphoreType.DMA((4,)),
            pltpu.SemaphoreType.DMA((copy_count,)),
            pltpu.SemaphoreType.DMA((copy_count,)),
        ],
        compiler_params=pltpu.CompilerParams(
            collective_id=number, has_side_effects=True, vmem_limit_bytes=55 * 2**20
        ),
    )(
        hidden_in,
        slot_choice.T,
        slot_expert.reshape(1, -1),
        norm_gain.reshape(1, -1),
        router_weight.T,
        slot_gate_up[0].transpose(1, 2, 0).reshape(2 * eff, feat),
        slot_down[0],
        shared_gate_up.transpose(1, 2, 0).reshape(2 * sff, feat),
        shared_down,
    )


def local_dense(
    hidden_in,
    norm_gain,
    router_weight,
    shared_gate_up,
    shared_down,
    slot_gate_up,
    slot_down,
    slot_expert,
    slot_choice,
    live_count,
):
    operands = (
        hidden_in,
        norm_gain,
        router_weight,
        shared_gate_up,
        shared_down,
        slot_gate_up,
        slot_down,
        slot_expert,
        slot_choice,
    )
    tok_count = hidden_in.shape[0]
    single = jnp.sum(slot_expert[:, None] == slot_expert[None, :], axis=1) == 1
    crowded = jnp.any(single[0::2] & single[1::2])
    mixed = lax.cond(
        crowded,
        functools.partial(local_plane, 96, 1),
        functools.partial(local_plane, 64, 0),
        *operands,
    )
    live_rows = jnp.arange(tok_count, dtype=jnp.int32) < live_count[0]
    return jnp.where(live_rows[:, None], mixed, jnp.zeros_like(mixed))


def solution(mesh):
    in_specs = (
        P("ep", "tp"),
        P(),
        P(),
        P(None, None, "tp"),
        P("tp", None),
        P(("ep", "tp"), None, None, None),
        P(("ep", "tp"), None, None),
        P(),
        P("ep", None),
        P("ep"),
    )
    out_specs = P("ep", "tp")
    small = mesh.size == 32 and mesh.shape["tp"] == 4
    local = local_dense if small else local_exchange
    return jax.shard_map(local, mesh=mesh, in_specs=in_specs, out_specs=out_specs, check_vma=False)
```

```python
import functools
import jax
import jax.numpy as jnp
from jax import lax
from jax.experimental import pallas as pl
from jax.experimental.pallas import tpu as pltpu
from jax.sharding import PartitionSpec as P


def gate_weights(normed_rows, choices, router_weight, slot_expert):
    logits = jnp.dot(normed_rows, router_weight, preferred_element_type=jnp.float32)
    slot_total = slot_expert.shape[0]
    expert_total = router_weight.shape[1]
    slot_hit = choices[:, :, None] == jnp.arange(slot_total, dtype=jnp.int32)
    expert_ids = jnp.sum(jnp.where(slot_hit, slot_expert, 0), axis=2)
    expert_hit = expert_ids[:, :, None] == jnp.arange(expert_total, dtype=jnp.int32)
    picked = jnp.sum(jnp.where(expert_hit, logits[:, None, :], 0.0), axis=2)
    highest = jnp.max(picked, axis=1, keepdims=True)
    weights = jnp.exp(picked - highest)
    return (weights / jnp.sum(weights, axis=1, keepdims=True)).astype(jnp.bfloat16)


def slot_positions(targets):
    length = targets.shape[0]
    same_slot = targets[:, None] == targets[None, :]
    earlier = jnp.arange(length)[None, :] < jnp.arange(length)[:, None]
    return jnp.sum(same_slot & earlier, axis=1)


def expert_apply(received, slot_gate_up, slot_down):
    shape_in = received.shape
    flat_rows = received.reshape(-1, shape_in[-1])
    gate_up = jnp.einsum(
        "rd,dgf->rgf", flat_rows, slot_gate_up[0], preferred_element_type=jnp.float32
    )
    activated = (jax.nn.silu(gate_up[:, 0]) * gate_up[:, 1]).astype(jnp.bfloat16)
    result = jnp.dot(activated, slot_down[0], preferred_element_type=jnp.float32).astype(
        jnp.bfloat16
    )
    return result.reshape(shape_in)


def local_exchange(
    hidden_in,
    norm_gain,
    router_weight,
    shared_gate_up,
    shared_down,
    slot_gate_up,
    slot_down,
    slot_expert,
    slot_choice,
    live_count,
):
    tp_count = lax.axis_size("tp")
    ep_count = lax.axis_size("ep")
    tp_index = lax.axis_index("tp")
    tok_count = hidden_in.shape[0]
    feature_width = hidden_in.shape[1] * tp_count
    top_count = slot_choice.shape[1]
    slot_count = slot_expert.shape[0]
    quarter = tok_count // tp_count
    capacity = max(2, 2 * quarter * top_count // slot_count)
    full_rows = lax.all_gather(hidden_in, "tp", axis=1, tiled=True)
    wide_rows = full_rows.astype(jnp.float32)
    norm_scale = lax.rsqrt(jnp.mean(wide_rows * wide_rows, axis=1, keepdims=True) + 1e-06)
    normed = (wide_rows * norm_scale * norm_gain).astype(jnp.bfloat16)
    shared_proj = jnp.einsum(
        "td,dgf->tgf", normed, shared_gate_up, preferred_element_type=jnp.float32
    )
    shared_hidden = (jax.nn.silu(shared_proj[:, 0]) * shared_proj[:, 1]).astype(jnp.bfloat16)
    partial_value = jnp.dot(shared_hidden, shared_down, preferred_element_type=jnp.float32)
    row_start = tp_index * quarter
    own_rows = lax.dynamic_slice_in_dim(normed, row_start, quarter, 0)
    own_choice = lax.dynamic_slice_in_dim(slot_choice, row_start, quarter, 0)
    gate_values = gate_weights(own_rows, own_choice, router_weight, slot_expert)
    targets = own_choice.reshape(-1)
    placed = targets * capacity + slot_positions(targets)
    outgoing = jnp.zeros((slot_count * capacity, feature_width), jnp.bfloat16)
    outgoing = outgoing.at[placed].set(jnp.repeat(own_rows, top_count, axis=0))
    outgoing = outgoing.reshape(ep_count, tp_count, capacity, feature_width)
    arrived = lax.all_to_all(
        lax.all_to_all(outgoing, "ep", split_axis=0, concat_axis=0, tiled=True),
        "tp",
        split_axis=1,
        concat_axis=1,
        tiled=True,
    )
    computed = expert_apply(arrived, slot_gate_up, slot_down)
    returned = lax.all_to_all(
        lax.all_to_all(computed, "ep", split_axis=0, concat_axis=0, tiled=True),
        "tp",
        split_axis=1,
        concat_axis=1,
        tiled=True,
    )
    fetched = returned.reshape(-1, feature_width)[placed].reshape(quarter, top_count, feature_width)
    routed = jnp.einsum("qk,qkd->qd", gate_values, fetched, preferred_element_type=jnp.float32)
    own_partial = lax.dynamic_slice_in_dim(partial_value, row_start, quarter, 0) + routed
    partial_value = lax.dynamic_update_slice_in_dim(partial_value, own_partial, row_start, 0)
    summed = lax.psum_scatter(partial_value, "tp", scatter_dimension=1, tiled=True)
    live_rows = jnp.arange(tok_count, dtype=jnp.int32) < live_count[0]
    mixed_out = jnp.where(live_rows[:, None], hidden_in.astype(jnp.float32) + summed, 0.0)
    return mixed_out.astype(jnp.bfloat16)


def dot_nt(a, b):
    return lax.dot_general(a, b, (((1,), (1,)), ((), ())), preferred_element_type=jnp.float32)


def dot_nn(a, b):
    return jnp.dot(a, b, preferred_element_type=jnp.float32)


def silu_mul(g, u):
    return (g / (1.0 + jnp.exp(-g)) * u).astype(jnp.bfloat16)


def chunks(total, step):
    return [(at, min(step, total - at)) for at in range(0, total, step)]


def plane_kernel(
    rows_max,
    slot_cap,
    top,
    hid,
    ch_own,
    slot_row,
    gain,
    router_t,
    w_gu,
    w_d,
    w_sgu,
    w_sd,
    out,
    zbuf,
    cz,
    gz,
    mz,
    shx,
    held,
    place,
    psel,
    sbuf,
    rbuf,
    gu,
    dn,
    sgu,
    sdn,
    own,
    hsh,
    shp,
    ssnd,
    srecv,
    sysnd,
    sy,
    sel,
    hmid,
    eo,
    ec,
    ro,
    ret,
    osum,
    rz,
    own_sum,
    wsem,
    ssem,
    rsem,
):
    bf16, f32 = jnp.bfloat16, jnp.float32
    ep, tp = lax.axis_index("ep"), lax.axis_index("tp")
    z, x, y, c = ep // 2, ep % 2, tp // 2, tp % 2
    tok, width = hid.shape
    feat = gain.shape[1]
    slots = slot_row.shape[1]
    experts_total = router_t.shape[0]
    reach = rows_max
    planes = (z, z + 1 - 2 * (z % 2), (z + 2) % 4, 3 - z)

    def at_ep(m, i):
        return planes[m] * 2 + (1 - x if i else x)

    def at_tp(k, l):
        return (1 - y if k else y) * 2 + (1 - c if l else c)

    def cols(k, l):
        return pl.ds(pl.multiple_of(at_tp(k, l) * width, width), width)

    chips = [(0, 0), (0, 1), (1, 0), (1, 1)]
    c_dev = (ep, at_tp(0, 1))
    chip_dev = {(i, k): (at_ep(0, i), at_tp(k, 0)) for i, k in chips}
    z_dev = [(at_ep(m, 0), tp) for m in range(4)]

    loads = [
        pltpu.make_async_copy(src, dst, wsem.at[n])
        for n, (src, dst) in enumerate(((w_sgu, sgu), (w_sd, sdn), (w_gu, gu), (w_d, dn)))
    ]
    barrier = pltpu.get_barrier_semaphore()
    greeted = [c_dev] + [chip_dev[q] for q in chips[1:]] + z_dev[1:]
    for dev in greeted:
        pl.semaphore_signal(barrier, inc=1, device_id=dev, device_id_type=pl.DeviceIdType.MESH)

    z_order = (1, 2, 3)
    copies = {}

    def send(name, src, dst, dev):
        n = len(copies)
        copy = pltpu.make_async_remote_copy(
            src_ref=src,
            dst_ref=dst,
            send_sem=ssem.at[n],
            recv_sem=rsem.at[n],
            device_id=dev,
            device_id_type=pl.DeviceIdType.MESH,
        )
        copy.start()
        copies[name] = copy

    def got(*name):
        copies[name].wait_recv()

    def one_hot(test):
        return jnp.where(test, 1.0, 0.0).astype(bf16)

    def tables():
        kind = lax.broadcasted_iota(jnp.int32, (experts_total, slots), 0)
        table = jnp.where(slot_row[...] == kind, 1.0, 0.0)
        copies_of = jnp.sum(table, axis=1, keepdims=True)
        single = jnp.sum(jnp.where(copies_of < 1.5, table, 0.0), axis=0, keepdims=True)
        a = lax.broadcasted_iota(jnp.int32, (slots, slots), 0)
        b = lax.broadcasted_iota(jnp.int32, (slots, slots), 1)
        single8 = jnp.broadcast_to(single, (8, slots))
        beside = dot_nn(single8.astype(bf16), one_hot(a == b + 1 - 2 * (b & 1)))
        share = jnp.where(
            single8 > 0.5,
            float(slot_cap),
            jnp.where(beside > 0.5, float(reach - slot_cap), float(reach // 2)),
        )
        table = table.astype(bf16)
        same = lax.dot_general(
            table, table, (((0,), (0,)), ((), ())), preferred_element_type=f32
        )
        first = dot_nn(share.astype(bf16), jnp.where(a < b, same, 0.0).astype(bf16))[0:1, :]
        share = share[0:1, :]
        slot = lax.broadcasted_iota(jnp.int32, (reach, slots), 1)
        start = jnp.where((slot & 1) == 1, float(reach) - share, 0.0)
        row = lax.broadcasted_iota(jnp.int32, (reach, slots), 0).astype(f32)
        inside = (row >= start) & (row < start + share)
        mine = None
        for n, (i, k) in enumerate(chips):
            even = at_ep(0, i) * 4 + (1 - y if k else y) * 2
            named = inside & ((slot == even) | (slot == even + 1))
            held[n * reach : (n + 1) * reach, :] = dot_nt(one_hot(named), table).astype(bf16)
            place[n * reach : (n + 1) * reach, :] = jnp.sum(
                jnp.where(named, first + row - start, 0.0), axis=1, keepdims=True
            )
            if n == 0:
                mine = jnp.sum(
                    jnp.where(named & (slot == even + c), 1.0, 0.0), axis=1, keepdims=True
                )
        return table, mine

    def choose(m, table):
        picks = ch_own[...] if m == 0 else cz[m]
        slot_ids = lax.broadcasted_iota(jnp.int32, (slots, tok), 0)
        named = jnp.zeros((slots, tok), f32)
        for k in range(top):
            named = jnp.where(picks[k : k + 1, :] == slot_ids, 1.0, named)
        times = dot_nn(table, named.astype(bf16))
        earlier = one_hot(
            lax.broadcasted_iota(jnp.int32, (tok, tok), 0)
            < lax.broadcasted_iota(jnp.int32, (tok, tok), 1)
        )
        rank = dot_nn(one_hot(times > 0.5), earlier)
        rank = jnp.where(times > 0.5, rank, -1.0).astype(bf16)
        mz[m] = times
        psel[m] = one_hot(dot_nn(held[...], rank) == place[...])

    def pick(m):
        src = hid if m == 0 else zbuf.at[m]
        for n in (1, 2, 3, 0):
            if m == 0 and n < 2:
                continue
            sbuf[m, n] = dot_nn(psel[m, n * reach : (n + 1) * reach, :], src[...]).astype(bf16)
            if m:
                ship(m, n)

    def ship(m, n):
        i, k = chips[n]
        if n:
            send(("g", m, n), sbuf.at[m, n], rbuf.at[m, n, 0], chip_dev[i, k])
        else:
            send(("gc", m, n), sbuf.at[m, 0], rbuf.at[m, 0, 1], c_dev)

    def norm_scale(*parts):
        squares = sum(jnp.sum(v * v, axis=1, keepdims=True) for v in parts)
        return lax.rsqrt(squares * (1.0 / feat) + 1e-06)

    def normed(refs, keep=None):
        parts = {kl: ref[...].astype(f32) for kl, ref in refs.items()}
        scale = norm_scale(*parts.values())
        if keep is not None:
            scale = scale * keep
        for (k, l), v in parts.items():
            yield k, l, (v * scale * gain[:, cols(k, l)]).astype(bf16)

    def own_rows():
        got("sc")
        got("sy")
        send(("syc",), shx.at[1], shx.at[2], c_dev)

    def own_norm():
        got("syc")
        for k, l, v in normed({(0, 0): hid, (0, 1): shx.at[0], (1, 0): shx.at[1], (1, 1): shx.at[2]}):
            own[:, cols(k, l)] = v

    def gates():
        logits = dot_nt(router_t[...], own[...])
        times = mz[0]
        there = times > 0.5
        top_logit = jnp.max(jnp.where(there, logits, -1e30), axis=0, keepdims=True)
        weights = jnp.where(there, jnp.exp(jnp.where(there, logits - top_logit, 0.0)), 0.0)
        total = jnp.sum(weights * times, axis=0, keepdims=True)
        gz[0] = (weights / total).astype(bf16).astype(f32)
        for m in (1, 2, 3):
            send(("gate", m), gz.at[0], gz.at[m], z_dev[m])

    def shared():
        loads[0].wait()
        ff = hsh.shape[1]
        hsh[...] = silu_mul(dot_nt(own[...], sgu[0:ff, :]), dot_nt(own[...], sgu[ff : 2 * ff, :]))
        loads[1].wait()
        for k in (0, 1):
            ssnd[k] = dot_nn(hsh[...], sdn[:, cols(k, 1)]).astype(bf16)
        send(("shc",), ssnd, srecv, c_dev)
        for k in (0, 1):
            shp[k] = dot_nn(hsh[...], sdn[:, cols(k, 0)])

    def shared_pass():
        got("shc")
        sysnd[...] = (shp[1] + srecv[1].astype(f32)).astype(bf16)
        send(("shy",), sysnd, sy, chip_dev[0, 1])
        own_sum[...] = hid[...].astype(f32) + shp[0] + srecv[0].astype(f32)

    def forward(m):
        for n in (1, 2, 3):
            if m == 0 and n == 1:
                continue
            got("g", m, n)
            send(("gc", m, n), rbuf.at[m, n, 0], rbuf.at[m, n, 1], c_dev)

    pos = {m: n for n, m in enumerate((1,2,3,0))}
    span = 2 * reach
    first_pass = (1, 2)

    def prepare(m, mine):
        for i in (0, 1):
            at = slice(pos[m] * span + i * reach, pos[m] * span + (i + 1) * reach)
            if m == 0 and i == 0:
                chosen = (psel[m, 0:reach, :].astype(f32) * mine).astype(bf16)
                for lo, size in chunks(feat, 512):
                    sel[at, lo : lo + size] = dot_nn(chosen, own[:, lo : lo + size]).astype(bf16)
                continue
            refs = {}
            for k in (0, 1):
                n = 2 * i + k
                refs[k, 0] = rbuf.at[m, n, 0] if n else sbuf.at[m, 0]
                got("gc", m, n)
                refs[k, 1] = rbuf.at[m, n, 1]
            for k, l, v in normed(refs, mine):
                sel[at, cols(k, l)] = v

    def experts(ms):
        part = slice(pos[ms[0]] * span, (pos[ms[-1]] + 1) * span)
        if ms == first_pass:
            loads[2].wait()
        ff = hmid.shape[1]
        for at, size in chunks(ff, 256):
            hmid[part, at : at + size] = silu_mul(
                dot_nt(sel[part, :], gu[at : at + size, :]),
                dot_nt(sel[part, :], gu[ff + at : ff + at + size, :]),
            )
        if ms == first_pass:
            loads[3].wait()
        for l in (1, 0):
            for k in (0, 1):
                value = dot_nn(hmid[part, :], dn[:, cols(k, l)]).astype(bf16)
                for n, m in enumerate(ms):
                    eo[m, l, k] = value[n * span : (n + 1) * span, :]
            if l:
                for m in ms:
                    send(("ec", m), eo.at[m, 1], ec.at[m], c_dev)

    def give_back(m):
        got("ec", m)
        for n in (3, 2, 1, 0):
            i, k = chips[n]
            at = slice(i * reach, (i + 1) * reach)
            value = eo[m, 0, k, at, :] + ec[m, k, at, :]
            if n:
                ro[m, n] = value
                send(("r", m, n), ro.at[m, n], ret.at[m, n], chip_dev[i, k])
            else:
                ret[m, 0] = value

    def collect(m):
        if m:
            got("gate", m)
        weight = dot_nn(held[...], gz[m].astype(bf16)) * dot_nn(held[...], mz[m].astype(bf16))
        weight = (weight * psel[m].astype(f32)).astype(bf16)
        for n in (1, 2, 3):
            got("r", m, n)
        part = lax.dot_general(
            weight,
            ret[m].reshape(4 * reach, width),
            (((0,), (0,)), ((), ())),
            preferred_element_type=f32,
        )
        if m:
            osum[m] = part.astype(bf16)
            send(("rz", m), osum.at[m], rz.at[m], z_dev[m])
        else:
            own_sum[...] += part

    for load in loads:
        load.start()
    table, mine = tables()
    choose(0, table)
    pick(0)
    pl.semaphore_wait(barrier, len(greeted))
    for m in z_order:
        send(("ch", m), ch_own, cz.at[m], z_dev[m])
    for m in z_order:
        send(("z", m), hid, zbuf.at[m], z_dev[m])
    send(("sy",), hid, shx.at[1], chip_dev[0, 1])
    send(("sc",), hid, shx.at[0], c_dev)
    ship(0, 3)
    ship(0, 2)
    for m in z_order:
        got("ch", m)
        choose(m, table)
    own_rows()
    got("z", 1)
    pick(1)
    own_norm()
    gates()
    shared()
    got("z", 2)
    pick(2)
    forward(0)
    shared_pass()
    prepare(0, mine)
    forward(1)
    prepare(1, mine)
    got("z", 3)
    pick(3)
    forward(2)
    prepare(2, mine)
    experts((1, 2))
    give_back(1)
    give_back(2)
    forward(3)
    prepare(3, mine)
    experts((3, 0))
    give_back(3)
    give_back(0)
    collect(1)
    collect(2)
    collect(3)
    collect(0)
    got("shy")
    for m in z_order:
        got("rz", m)
    total = own_sum[...] + sy[...].astype(f32)
    for m in z_order:
        total = total + rz[m].astype(f32)
    out[...] = total.astype(bf16)
    for copy in copies.values():
        copy.wait_send()


def local_plane(
    rows_max,
    number,
    hidden_in,
    norm_gain,
    router_weight,
    shared_gate_up,
    shared_down,
    slot_gate_up,
    slot_down,
    slot_expert,
    slot_choice,
):
    tok_count, width = hidden_in.shape
    feat = 4 * width
    top_count = slot_choice.shape[1]
    slot_count = slot_expert.shape[0]
    expert_count = router_weight.shape[1]
    cap = 4 * max(2, 2 * (tok_count // 4) * top_count // slot_count)
    sff, eff = shared_down.shape[0], slot_down.shape[1]
    bf16, f32 = jnp.bfloat16, jnp.float32
    block = (tok_count, width)
    piece = (rows_max, width)
    vmem = pl.BlockSpec(memory_space=pltpu.VMEM)
    hbm = pl.BlockSpec(memory_space=pl.ANY)
    copy_count = 61
    return pl.pallas_call(
        functools.partial(plane_kernel, rows_max, cap, top_count),
        out_shape=jax.ShapeDtypeStruct(block, bf16),
        in_specs=[vmem] * 5 + [hbm] * 4,
        out_specs=vmem,
        scratch_shapes=[
            pltpu.VMEM((4,) + block, bf16),
            pltpu.VMEM((4, top_count, tok_count), jnp.int32),
            pltpu.VMEM((4, expert_count, tok_count), f32),
            pltpu.VMEM((4, expert_count, tok_count), f32),
            pltpu.VMEM((3,) + block, bf16),
            pltpu.VMEM((4 * rows_max, expert_count), bf16),
            pltpu.VMEM((4 * rows_max, 1), f32),
            pltpu.VMEM((4, 4 * rows_max, tok_count), bf16),
            pltpu.VMEM((4, 4) + piece, bf16),
            pltpu.VMEM((4, 4, 2) + piece, bf16),
            pltpu.VMEM((2 * eff, feat), bf16),
            pltpu.VMEM((eff, feat), bf16),
            pltpu.VMEM((2 * sff, feat), bf16),
            pltpu.VMEM((sff, feat), bf16),
            pltpu.VMEM((tok_count, feat), bf16),
            pltpu.VMEM((tok_count, sff), bf16),
            pltpu.VMEM((2,) + block, f32),
            pltpu.VMEM((2,) + block, bf16),
            pltpu.VMEM((2,) + block, bf16),
            pltpu.VMEM(block, bf16),
            pltpu.VMEM(block, bf16),
            pltpu.VMEM((8 * rows_max, feat), bf16),
            pltpu.VMEM((8 * rows_max, eff), bf16),
            pltpu.VMEM((4, 2, 2, 2 * rows_max, width), bf16),
            pltpu.VMEM((4, 2, 2 * rows_max, width), bf16),
            pltpu.VMEM((4, 4) + piece, bf16),
            pltpu.VMEM((4, 4) + piece, bf16),
            pltpu.VMEM((4,) + block, bf16),
            pltpu.VMEM((4,) + block, bf16),
            pltpu.VMEM(block, f32),
            pltpu.SemaphoreType.DMA((4,)),
            pltpu.SemaphoreType.DMA((copy_count,)),
            pltpu.SemaphoreType.DMA((copy_count,)),
        ],
        compiler_params=pltpu.CompilerParams(
            collective_id=number, has_side_effects=True, vmem_limit_bytes=55 * 2**20
        ),
    )(
        hidden_in,
        slot_choice.T,
        slot_expert.reshape(1, -1),
        norm_gain.reshape(1, -1),
        router_weight.T,
        slot_gate_up[0].transpose(1, 2, 0).reshape(2 * eff, feat),
        slot_down[0],
        shared_gate_up.transpose(1, 2, 0).reshape(2 * sff, feat),
        shared_down,
    )


def local_dense(
    hidden_in,
    norm_gain,
    router_weight,
    shared_gate_up,
    shared_down,
    slot_gate_up,
    slot_down,
    slot_expert,
    slot_choice,
    live_count,
):
    operands = (
        hidden_in,
        norm_gain,
        router_weight,
        shared_gate_up,
        shared_down,
        slot_gate_up,
        slot_down,
        slot_expert,
        slot_choice,
    )
    tok_count = hidden_in.shape[0]
    single = jnp.sum(slot_expert[:, None] == slot_expert[None, :], axis=1) == 1
    crowded = jnp.any(single[0::2] & single[1::2])
    mixed = lax.cond(
        crowded,
        functools.partial(local_plane, 96, 1),
        functools.partial(local_plane, 64, 0),
        *operands,
    )
    live_rows = jnp.arange(tok_count, dtype=jnp.int32) < live_count[0]
    return jnp.where(live_rows[:, None], mixed, jnp.zeros_like(mixed))


def solution(mesh):
    in_specs = (
        P("ep", "tp"),
        P(),
        P(),
        P(None, None, "tp"),
        P("tp", None),
        P(("ep", "tp"), None, None, None),
        P(("ep", "tp"), None, None),
        P(),
        P("ep", None),
        P("ep"),
    )
    out_specs = P("ep", "tp")
    small = mesh.size == 32 and mesh.shape["tp"] == 4
    local = local_dense if small else local_exchange
    return jax.shard_map(local, mesh=mesh, in_specs=in_specs, out_specs=out_specs, check_vma=False)
```

```python
import functools
import jax
import jax.numpy as jnp
from jax import lax
from jax.experimental import pallas as pl
from jax.experimental.pallas import tpu as pltpu
from jax.sharding import PartitionSpec as P


def gate_weights(normed_rows, choices, router_weight, slot_expert):
    logits = jnp.dot(normed_rows, router_weight, preferred_element_type=jnp.float32)
    slot_total = slot_expert.shape[0]
    expert_total = router_weight.shape[1]
    slot_hit = choices[:, :, None] == jnp.arange(slot_total, dtype=jnp.int32)
    expert_ids = jnp.sum(jnp.where(slot_hit, slot_expert, 0), axis=2)
    expert_hit = expert_ids[:, :, None] == jnp.arange(expert_total, dtype=jnp.int32)
    picked = jnp.sum(jnp.where(expert_hit, logits[:, None, :], 0.0), axis=2)
    highest = jnp.max(picked, axis=1, keepdims=True)
    weights = jnp.exp(picked - highest)
    return (weights / jnp.sum(weights, axis=1, keepdims=True)).astype(jnp.bfloat16)


def slot_positions(targets):
    length = targets.shape[0]
    same_slot = targets[:, None] == targets[None, :]
    earlier = jnp.arange(length)[None, :] < jnp.arange(length)[:, None]
    return jnp.sum(same_slot & earlier, axis=1)


def expert_apply(received, slot_gate_up, slot_down):
    shape_in = received.shape
    flat_rows = received.reshape(-1, shape_in[-1])
    gate_up = jnp.einsum(
        "rd,dgf->rgf", flat_rows, slot_gate_up[0], preferred_element_type=jnp.float32
    )
    activated = (jax.nn.silu(gate_up[:, 0]) * gate_up[:, 1]).astype(jnp.bfloat16)
    result = jnp.dot(activated, slot_down[0], preferred_element_type=jnp.float32).astype(
        jnp.bfloat16
    )
    return result.reshape(shape_in)


def local_exchange(
    hidden_in,
    norm_gain,
    router_weight,
    shared_gate_up,
    shared_down,
    slot_gate_up,
    slot_down,
    slot_expert,
    slot_choice,
    live_count,
):
    tp_count = lax.axis_size("tp")
    ep_count = lax.axis_size("ep")
    tp_index = lax.axis_index("tp")
    tok_count = hidden_in.shape[0]
    feature_width = hidden_in.shape[1] * tp_count
    top_count = slot_choice.shape[1]
    slot_count = slot_expert.shape[0]
    quarter = tok_count // tp_count
    capacity = max(2, 2 * quarter * top_count // slot_count)
    full_rows = lax.all_gather(hidden_in, "tp", axis=1, tiled=True)
    wide_rows = full_rows.astype(jnp.float32)
    norm_scale = lax.rsqrt(jnp.mean(wide_rows * wide_rows, axis=1, keepdims=True) + 1e-06)
    normed = (wide_rows * norm_scale * norm_gain).astype(jnp.bfloat16)
    shared_proj = jnp.einsum(
        "td,dgf->tgf", normed, shared_gate_up, preferred_element_type=jnp.float32
    )
    shared_hidden = (jax.nn.silu(shared_proj[:, 0]) * shared_proj[:, 1]).astype(jnp.bfloat16)
    partial_value = jnp.dot(shared_hidden, shared_down, preferred_element_type=jnp.float32)
    row_start = tp_index * quarter
    own_rows = lax.dynamic_slice_in_dim(normed, row_start, quarter, 0)
    own_choice = lax.dynamic_slice_in_dim(slot_choice, row_start, quarter, 0)
    gate_values = gate_weights(own_rows, own_choice, router_weight, slot_expert)
    targets = own_choice.reshape(-1)
    placed = targets * capacity + slot_positions(targets)
    outgoing = jnp.zeros((slot_count * capacity, feature_width), jnp.bfloat16)
    outgoing = outgoing.at[placed].set(jnp.repeat(own_rows, top_count, axis=0))
    outgoing = outgoing.reshape(ep_count, tp_count, capacity, feature_width)
    arrived = lax.all_to_all(
        lax.all_to_all(outgoing, "ep", split_axis=0, concat_axis=0, tiled=True),
        "tp",
        split_axis=1,
        concat_axis=1,
        tiled=True,
    )
    computed = expert_apply(arrived, slot_gate_up, slot_down)
    returned = lax.all_to_all(
        lax.all_to_all(computed, "ep", split_axis=0, concat_axis=0, tiled=True),
        "tp",
        split_axis=1,
        concat_axis=1,
        tiled=True,
    )
    fetched = returned.reshape(-1, feature_width)[placed].reshape(quarter, top_count, feature_width)
    routed = jnp.einsum("qk,qkd->qd", gate_values, fetched, preferred_element_type=jnp.float32)
    own_partial = lax.dynamic_slice_in_dim(partial_value, row_start, quarter, 0) + routed
    partial_value = lax.dynamic_update_slice_in_dim(partial_value, own_partial, row_start, 0)
    summed = lax.psum_scatter(partial_value, "tp", scatter_dimension=1, tiled=True)
    live_rows = jnp.arange(tok_count, dtype=jnp.int32) < live_count[0]
    mixed_out = jnp.where(live_rows[:, None], hidden_in.astype(jnp.float32) + summed, 0.0)
    return mixed_out.astype(jnp.bfloat16)


def dot_nt(a, b):
    return lax.dot_general(a, b, (((1,), (1,)), ((), ())), preferred_element_type=jnp.float32)


def dot_nn(a, b):
    return jnp.dot(a, b, preferred_element_type=jnp.float32)


def silu_mul(g, u):
    return (g / (1.0 + jnp.exp(-g)) * u).astype(jnp.bfloat16)


def chunks(total, step):
    return [(at, min(step, total - at)) for at in range(0, total, step)]


def plane_kernel(
    rows_max,
    slot_cap,
    top,
    hid,
    ch_own,
    slot_row,
    gain,
    router_t,
    w_gu,
    w_d,
    w_sgu,
    w_sd,
    out,
    zbuf,
    cz,
    gz,
    mz,
    shx,
    held,
    place,
    psel,
    sbuf,
    rbuf,
    gu,
    dn,
    sgu,
    sdn,
    own,
    hsh,
    shp,
    ssnd,
    srecv,
    sysnd,
    sy,
    sel,
    hmid,
    eo,
    ec,
    ro,
    ret,
    osum,
    rz,
    own_sum,
    wsem,
    ssem,
    rsem,
):
    bf16, f32 = jnp.bfloat16, jnp.float32
    ep, tp = lax.axis_index("ep"), lax.axis_index("tp")
    z, x, y, c = ep // 2, ep % 2, tp // 2, tp % 2
    tok, width = hid.shape
    feat = gain.shape[1]
    slots = slot_row.shape[1]
    experts_total = router_t.shape[0]
    reach = rows_max
    planes = (z, z + 1 - 2 * (z % 2), (z + 2) % 4, 3 - z)

    def at_ep(m, i):
        return planes[m] * 2 + (1 - x if i else x)

    def at_tp(k, l):
        return (1 - y if k else y) * 2 + (1 - c if l else c)

    def cols(k, l):
        return pl.ds(pl.multiple_of(at_tp(k, l) * width, width), width)

    chips = [(0, 0), (0, 1), (1, 0), (1, 1)]
    c_dev = (ep, at_tp(0, 1))
    chip_dev = {(i, k): (at_ep(0, i), at_tp(k, 0)) for i, k in chips}
    z_dev = [(at_ep(m, 0), tp) for m in range(4)]

    loads = [
        pltpu.make_async_copy(src, dst, wsem.at[n])
        for n, (src, dst) in enumerate(((w_sgu, sgu), (w_sd, sdn), (w_gu, gu), (w_d, dn)))
    ]
    barrier = pltpu.get_barrier_semaphore()
    greeted = [c_dev] + [chip_dev[q] for q in chips[1:]] + z_dev[1:]
    for dev in greeted:
        pl.semaphore_signal(barrier, inc=1, device_id=dev, device_id_type=pl.DeviceIdType.MESH)

    z_order = (1, 2, 3)
    copies = {}

    def send(name, src, dst, dev):
        n = len(copies)
        copy = pltpu.make_async_remote_copy(
            src_ref=src,
            dst_ref=dst,
            send_sem=ssem.at[n],
            recv_sem=rsem.at[n],
            device_id=dev,
            device_id_type=pl.DeviceIdType.MESH,
        )
        copy.start()
        copies[name] = copy

    def got(*name):
        copies[name].wait_recv()

    def one_hot(test):
        return jnp.where(test, 1.0, 0.0).astype(bf16)

    def tables():
        kind = lax.broadcasted_iota(jnp.int32, (experts_total, slots), 0)
        table = jnp.where(slot_row[...] == kind, 1.0, 0.0)
        copies_of = jnp.sum(table, axis=1, keepdims=True)
        single = jnp.sum(jnp.where(copies_of < 1.5, table, 0.0), axis=0, keepdims=True)
        a = lax.broadcasted_iota(jnp.int32, (slots, slots), 0)
        b = lax.broadcasted_iota(jnp.int32, (slots, slots), 1)
        single8 = jnp.broadcast_to(single, (8, slots))
        beside = dot_nn(single8.astype(bf16), one_hot(a == b + 1 - 2 * (b & 1)))
        share = jnp.where(
            single8 > 0.5,
            float(slot_cap),
            jnp.where(beside > 0.5, float(reach - slot_cap), float(reach // 2)),
        )
        table = table.astype(bf16)
        same = lax.dot_general(
            table, table, (((0,), (0,)), ((), ())), preferred_element_type=f32
        )
        first = dot_nn(share.astype(bf16), jnp.where(a < b, same, 0.0).astype(bf16))[0:1, :]
        share = share[0:1, :]
        slot = lax.broadcasted_iota(jnp.int32, (reach, slots), 1)
        start = jnp.where((slot & 1) == 1, float(reach) - share, 0.0)
        row = lax.broadcasted_iota(jnp.int32, (reach, slots), 0).astype(f32)
        inside = (row >= start) & (row < start + share)
        mine = None
        for n, (i, k) in enumerate(chips):
            even = at_ep(0, i) * 4 + (1 - y if k else y) * 2
            named = inside & ((slot == even) | (slot == even + 1))
            held[n * reach : (n + 1) * reach, :] = dot_nt(one_hot(named), table).astype(bf16)
            place[n * reach : (n + 1) * reach, :] = jnp.sum(
                jnp.where(named, first + row - start, 0.0), axis=1, keepdims=True
            )
            if n == 0:
                mine = jnp.sum(
                    jnp.where(named & (slot == even + c), 1.0, 0.0), axis=1, keepdims=True
                )
        return table, mine

    def choose(m, table):
        picks = ch_own[...] if m == 0 else cz[m]
        slot_ids = lax.broadcasted_iota(jnp.int32, (slots, tok), 0)
        named = jnp.zeros((slots, tok), f32)
        for k in range(top):
            named = jnp.where(picks[k : k + 1, :] == slot_ids, 1.0, named)
        times = dot_nn(table, named.astype(bf16))
        earlier = one_hot(
            lax.broadcasted_iota(jnp.int32, (tok, tok), 0)
            < lax.broadcasted_iota(jnp.int32, (tok, tok), 1)
        )
        rank = dot_nn(one_hot(times > 0.5), earlier)
        rank = jnp.where(times > 0.5, rank, -1.0).astype(bf16)
        mz[m] = times
        psel[m] = one_hot(dot_nn(held[...], rank) == place[...])

    def pick(m):
        src = hid if m == 0 else zbuf.at[m]
        for n in (1, 2, 3, 0):
            if m == 0 and n < 2:
                continue
            sbuf[m, n] = dot_nn(psel[m, n * reach : (n + 1) * reach, :], src[...]).astype(bf16)
            if m:
                ship(m, n)

    def ship(m, n):
        i, k = chips[n]
        if n:
            send(("g", m, n), sbuf.at[m, n], rbuf.at[m, n, 0], chip_dev[i, k])
        else:
            send(("gc", m, n), sbuf.at[m, 0], rbuf.at[m, 0, 1], c_dev)

    def norm_scale(*parts):
        squares = sum(jnp.sum(v * v, axis=1, keepdims=True) for v in parts)
        return lax.rsqrt(squares * (1.0 / feat) + 1e-06)

    def normed(refs, keep=None):
        parts = {kl: ref[...].astype(f32) for kl, ref in refs.items()}
        scale = norm_scale(*parts.values())
        if keep is not None:
            scale = scale * keep
        for (k, l), v in parts.items():
            yield k, l, (v * scale * gain[:, cols(k, l)]).astype(bf16)

    def own_rows():
        got("sc")
        got("sy")
        send(("syc",), shx.at[1], shx.at[2], c_dev)

    def own_norm():
        got("syc")
        for k, l, v in normed({(0, 0): hid, (0, 1): shx.at[0], (1, 0): shx.at[1], (1, 1): shx.at[2]}):
            own[:, cols(k, l)] = v

    def gates():
        logits = dot_nt(router_t[...], own[...])
        times = mz[0]
        there = times > 0.5
        top_logit = jnp.max(jnp.where(there, logits, -1e30), axis=0, keepdims=True)
        weights = jnp.where(there, jnp.exp(jnp.where(there, logits - top_logit, 0.0)), 0.0)
        total = jnp.sum(weights * times, axis=0, keepdims=True)
        gz[0] = (weights / total).astype(bf16).astype(f32)
        for m in (1, 2, 3):
            send(("gate", m), gz.at[0], gz.at[m], z_dev[m])

    def shared():
        loads[0].wait()
        ff = hsh.shape[1]
        hsh[...] = silu_mul(dot_nt(own[...], sgu[0:ff, :]), dot_nt(own[...], sgu[ff : 2 * ff, :]))
        loads[1].wait()
        for k in (0, 1):
            ssnd[k] = dot_nn(hsh[...], sdn[:, cols(k, 1)]).astype(bf16)
        send(("shc",), ssnd, srecv, c_dev)
        for k in (0, 1):
            shp[k] = dot_nn(hsh[...], sdn[:, cols(k, 0)])

    def shared_pass():
        got("shc")
        sysnd[...] = (shp[1] + srecv[1].astype(f32)).astype(bf16)
        send(("shy",), sysnd, sy, chip_dev[0, 1])
        own_sum[...] = hid[...].astype(f32) + shp[0] + srecv[0].astype(f32)

    def forward(m):
        for n in (1, 2, 3):
            if m == 0 and n == 1:
                continue
            got("g", m, n)
            send(("gc", m, n), rbuf.at[m, n, 0], rbuf.at[m, n, 1], c_dev)

    pos = {m: n for n, m in enumerate((1,2,3,0))}
    span = 2 * reach
    first_pass = (1, 2)

    def prepare(m, mine):
        for i in (0, 1):
            at = slice(pos[m] * span + i * reach, pos[m] * span + (i + 1) * reach)
            if m == 0 and i == 0:
                chosen = (psel[m, 0:reach, :].astype(f32) * mine).astype(bf16)
                for lo, size in chunks(feat, 512):
                    sel[at, lo : lo + size] = dot_nn(chosen, own[:, lo : lo + size]).astype(bf16)
                continue
            refs = {}
            for k in (0, 1):
                n = 2 * i + k
                refs[k, 0] = rbuf.at[m, n, 0] if n else sbuf.at[m, 0]
                got("gc", m, n)
                refs[k, 1] = rbuf.at[m, n, 1]
            for k, l, v in normed(refs, mine):
                sel[at, cols(k, l)] = v

    def experts(ms):
        part = slice(pos[ms[0]] * span, (pos[ms[-1]] + 1) * span)
        if ms == first_pass:
            loads[2].wait()
        ff = hmid.shape[1]
        for at, size in chunks(ff, 256):
            hmid[part, at : at + size] = silu_mul(
                dot_nt(sel[part, :], gu[at : at + size, :]),
                dot_nt(sel[part, :], gu[ff + at : ff + at + size, :]),
            )
        if ms == first_pass:
            loads[3].wait()
        for l in (1, 0):
            for k in (0, 1):
                value = dot_nn(hmid[part, :], dn[:, cols(k, l)]).astype(bf16)
                for n, m in enumerate(ms):
                    eo[m, l, k] = value[n * span : (n + 1) * span, :]
            if l:
                for m in ms:
                    send(("ec", m), eo.at[m, 1], ec.at[m], c_dev)

    def give_back(m):
        got("ec", m)
        for n in (3, 2, 1, 0):
            i, k = chips[n]
            at = slice(i * reach, (i + 1) * reach)
            value = eo[m, 0, k, at, :] + ec[m, k, at, :]
            if n:
                ro[m, n] = value
                send(("r", m, n), ro.at[m, n], ret.at[m, n], chip_dev[i, k])
            else:
                ret[m, 0] = value

    def collect(m):
        if m:
            got("gate", m)
        weight = dot_nn(held[...], gz[m].astype(bf16)) * dot_nn(held[...], mz[m].astype(bf16))
        weight = (weight * psel[m].astype(f32)).astype(bf16)
        for n in (1, 2, 3):
            got("r", m, n)
        part = lax.dot_general(
            weight,
            ret[m].reshape(4 * reach, width),
            (((0,), (0,)), ((), ())),
            preferred_element_type=f32,
        )
        if m:
            osum[m] = part.astype(bf16)
            send(("rz", m), osum.at[m], rz.at[m], z_dev[m])
        else:
            own_sum[...] += part

    for load in loads:
        load.start()
    table, mine = tables()
    choose(0, table)
    pick(0)
    pl.semaphore_wait(barrier, len(greeted))
    for m in z_order:
        send(("ch", m), ch_own, cz.at[m], z_dev[m])
    for m in z_order:
        send(("z", m), hid, zbuf.at[m], z_dev[m])
    send(("sy",), hid, shx.at[1], chip_dev[0, 1])
    send(("sc",), hid, shx.at[0], c_dev)
    ship(0, 3)
    ship(0, 2)
    for m in z_order:
        got("ch", m)
        choose(m, table)
    own_rows()
    got("z", 1)
    pick(1)
    own_norm()
    gates()
    shared()
    got("z", 2)
    pick(2)
    forward(0)
    shared_pass()
    prepare(0, mine)
    forward(1)
    prepare(1, mine)
    got("z", 3)
    pick(3)
    forward(2)
    prepare(2, mine)
    experts((1, 2))
    give_back(1)
    give_back(2)
    forward(3)
    prepare(3, mine)
    experts((3, 0))
    give_back(3)
    collect(1)
    collect(2)
    give_back(0)
    collect(3)
    collect(0)
    got("shy")
    for m in z_order:
        got("rz", m)
    total = own_sum[...] + sy[...].astype(f32)
    for m in z_order:
        total = total + rz[m].astype(f32)
    out[...] = total.astype(bf16)
    for copy in copies.values():
        copy.wait_send()


def local_plane(
    rows_max,
    number,
    hidden_in,
    norm_gain,
    router_weight,
    shared_gate_up,
    shared_down,
    slot_gate_up,
    slot_down,
    slot_expert,
    slot_choice,
):
    tok_count, width = hidden_in.shape
    feat = 4 * width
    top_count = slot_choice.shape[1]
    slot_count = slot_expert.shape[0]
    expert_count = router_weight.shape[1]
    cap = 4 * max(2, 2 * (tok_count // 4) * top_count // slot_count)
    sff, eff = shared_down.shape[0], slot_down.shape[1]
    bf16, f32 = jnp.bfloat16, jnp.float32
    block = (tok_count, width)
    piece = (rows_max, width)
    vmem = pl.BlockSpec(memory_space=pltpu.VMEM)
    hbm = pl.BlockSpec(memory_space=pl.ANY)
    copy_count = 61
    return pl.pallas_call(
        functools.partial(plane_kernel, rows_max, cap, top_count),
        out_shape=jax.ShapeDtypeStruct(block, bf16),
        in_specs=[vmem] * 5 + [hbm] * 4,
        out_specs=vmem,
        scratch_shapes=[
            pltpu.VMEM((4,) + block, bf16),
            pltpu.VMEM((4, top_count, tok_count), jnp.int32),
            pltpu.VMEM((4, expert_count, tok_count), f32),
            pltpu.VMEM((4, expert_count, tok_count), f32),
            pltpu.VMEM((3,) + block, bf16),
            pltpu.VMEM((4 * rows_max, expert_count), bf16),
            pltpu.VMEM((4 * rows_max, 1), f32),
            pltpu.VMEM((4, 4 * rows_max, tok_count), bf16),
            pltpu.VMEM((4, 4) + piece, bf16),
            pltpu.VMEM((4, 4, 2) + piece, bf16),
            pltpu.VMEM((2 * eff, feat), bf16),
            pltpu.VMEM((eff, feat), bf16),
            pltpu.VMEM((2 * sff, feat), bf16),
            pltpu.VMEM((sff, feat), bf16),
            pltpu.VMEM((tok_count, feat), bf16),
            pltpu.VMEM((tok_count, sff), bf16),
            pltpu.VMEM((2,) + block, f32),
            pltpu.VMEM((2,) + block, bf16),
            pltpu.VMEM((2,) + block, bf16),
            pltpu.VMEM(block, bf16),
            pltpu.VMEM(block, bf16),
            pltpu.VMEM((8 * rows_max, feat), bf16),
            pltpu.VMEM((8 * rows_max, eff), bf16),
            pltpu.VMEM((4, 2, 2, 2 * rows_max, width), bf16),
            pltpu.VMEM((4, 2, 2 * rows_max, width), bf16),
            pltpu.VMEM((4, 4) + piece, bf16),
            pltpu.VMEM((4, 4) + piece, bf16),
            pltpu.VMEM((4,) + block, bf16),
            pltpu.VMEM((4,) + block, bf16),
            pltpu.VMEM(block, f32),
            pltpu.SemaphoreType.DMA((4,)),
            pltpu.SemaphoreType.DMA((copy_count,)),
            pltpu.SemaphoreType.DMA((copy_count,)),
        ],
        compiler_params=pltpu.CompilerParams(
            collective_id=number, has_side_effects=True, vmem_limit_bytes=55 * 2**20
        ),
    )(
        hidden_in,
        slot_choice.T,
        slot_expert.reshape(1, -1),
        norm_gain.reshape(1, -1),
        router_weight.T,
        slot_gate_up[0].transpose(1, 2, 0).reshape(2 * eff, feat),
        slot_down[0],
        shared_gate_up.transpose(1, 2, 0).reshape(2 * sff, feat),
        shared_down,
    )


def local_dense(
    hidden_in,
    norm_gain,
    router_weight,
    shared_gate_up,
    shared_down,
    slot_gate_up,
    slot_down,
    slot_expert,
    slot_choice,
    live_count,
):
    operands = (
        hidden_in,
        norm_gain,
        router_weight,
        shared_gate_up,
        shared_down,
        slot_gate_up,
        slot_down,
        slot_expert,
        slot_choice,
    )
    tok_count = hidden_in.shape[0]
    single = jnp.sum(slot_expert[:, None] == slot_expert[None, :], axis=1) == 1
    crowded = jnp.any(single[0::2] & single[1::2])
    mixed = lax.cond(
        crowded,
        functools.partial(local_plane, 96, 1),
        functools.partial(local_plane, 64, 0),
        *operands,
    )
    live_rows = jnp.arange(tok_count, dtype=jnp.int32) < live_count[0]
    return jnp.where(live_rows[:, None], mixed, jnp.zeros_like(mixed))


def solution(mesh):
    in_specs = (
        P("ep", "tp"),
        P(),
        P(),
        P(None, None, "tp"),
        P("tp", None),
        P(("ep", "tp"), None, None, None),
        P(("ep", "tp"), None, None),
        P(),
        P("ep", None),
        P("ep"),
    )
    out_specs = P("ep", "tp")
    small = mesh.size == 32 and mesh.shape["tp"] == 4
    local = local_dense if small else local_exchange
    return jax.shard_map(local, mesh=mesh, in_specs=in_specs, out_specs=out_specs, check_vma=False)
```
